32 devices in a mesh: section: 4 (over y, x), scen: 8 (over z, core).
Axes of the slice: x: 2, y: 2, z: 4, core: 2. Of those that a mesh axis runs over, the one named last changes fastest.
Arguments:
- right_side: float32 [4, 8, 512, 1024], P('section', 'scen'), may hold values from -6 to 6
- inverse_raw: bfloat16 [4, 8, 1024, 1024], P('section', 'scen'), may hold values from -0.1875 to 0.1875
- inverse_pattern: int32 [4, 8, 16, 16], P('section', 'scen'), may hold values 0 or 1
- coupling: bfloat16 [4, 8, 1024, 1024], P('section', 'scen'), may hold values from -0.1875 to 0.1875
- coupling_pattern: int32 [4, 8, 16, 16], P('section', 'scen'), may hold values 0 or 1
- pivots: float32 [4, 8, 1024], P('section', 'scen'), may hold values from 0.5 to 2
- offsets: int32 [4, 8], replicated, may hold values from 0 to 1, as said below
- above_solution: bfloat16 [8, 512, 1024], P('scen'), may hold values from -6 to 6
Outputs:
- solution: float32 [4, 8, 512, 1024], P('section', 'scen')
The draws below stay inside these ranges and needn't reach their ends.
Inputs may be any that keep to these rules, and one draw needn't show every extreme that they name: Node c of level l has node c + offsets[l, c] of level l - 1 as its parent, and for l = 0 row c + offsets[0, c] of above_solution; offsets[l, 0] is 1 and offsets[l, 7] is 0 for every l.
All inputs are finite; a program needn't handle non-finite values. No bound on the sum of `inverse_pattern` or of `coupling_pattern` on one device may be relied on, other than what follows from the above.
Results may differ from the reference program's by a relative error of at most 0.0075.
Values may be sent and summed in bfloat16 or wider, within the bound.
A program may use at most 64 MiB of HBM per device.

```python
import math
import jax
import jax.numpy as jnp
from jax import lax

NA = 1024
NB = 16
COLS = 512
LEVELS = 4
NODES = 8


def draw_offsets(key, part):
    picked = jax.random.randint(key, (LEVELS, NODES), 0, 2)
    col_ids = jnp.arange(NODES)[None, :]
    middle = NODES // 2
    picked = jnp.where((col_ids >= middle - 2) & (col_ids <= middle), 1, picked)
    picked = jnp.where(col_ids == 0, 1, picked)
    return jnp.where(col_ids == NODES - 1, 0, picked).astype(jnp.int32)


def set_ends(values, stream_key, least, high):
    longest = values.shape.index(max(values.shape))
    spots = []
    for shift in (0, 1):
        where = [jax.random.randint(jax.random.fold_in(stream_key, axis), (), 0, length) for axis, length in enumerate(values.shape)]
        where[longest] = (where[longest] + shift) % values.shape[longest]
        spots.append(tuple(where))
    return values.at[spots[0]].set(least).at[spots[1]].set(high)


def block_levels(rng, extent, pieces, low, largest):
    level = 1.0
    for position, shards_of in pieces:
        steps = jax.random.uniform(jax.random.fold_in(jax.random.fold_in(rng, 6), position), (shards_of,), jnp.float32, low / len(pieces), largest / len(pieces))
        level = level * jnp.repeat(jnp.exp(steps), extent[position] // shards_of).reshape((-1,) + (1,) * (len(extent) - 1 - position))
    return level


def noise(own_key, shape, scale, most, pieces=(), dtype=jnp.bfloat16):
    entries = scale * jax.random.normal(own_key, shape, jnp.float32)
    if pieces:
        entries = entries * block_levels(own_key, shape, pieces, -0.22, 0.18)
    return jnp.clip(entries, -most, most).astype(dtype)


def setup_inputs(seed: int = 0) -> dict:
    key_of = jax.random.split(jax.random.key(seed), 9)
    right_side = noise(key_of[0], (LEVELS, NODES, COLS, NA), 1.0, 6.0, ((0, 4), (1, 8)), jnp.float32)
    inverse_raw = noise(key_of[1], (LEVELS, NODES, NA, NA), NA ** -0.5, 0.1875, ((0, 4), (1, 8)))
    inverse_pattern = set_ends((jax.random.randint(key_of[2], (LEVELS, NODES, NB, NB), 0, 2) < 1).astype(jnp.int32), jax.random.fold_in(key_of[2], 1), 0, 1)
    coupling = noise(key_of[3], (LEVELS, NODES, NA, NA), NA ** -0.5, 0.1875, ((0, 4), (1, 8)))
    coupling_pattern = set_ends((jax.random.randint(key_of[4], (LEVELS, NODES, NB, NB), 0, 2) < 1).astype(jnp.int32), jax.random.fold_in(key_of[4], 1), 0, 1)
    pivots = jnp.clip(jnp.exp(math.log(2.0) - 1.3862944 * jax.random.uniform(key_of[5], (LEVELS, NODES, NA), jnp.float32) ** block_levels(key_of[5], (LEVELS, NODES, NA), ((0, 4), (1, 8)), -0.2, 0.2)), 0.5, 2.0)
    offsets = draw_offsets(jax.random.fold_in(key_of[8], 71), 0)
    above_solution = noise(key_of[7], (NODES, COLS, NA), 1.0, 6.0, ((0, 8),))
    return dict(right_side=right_side, inverse_raw=inverse_raw, inverse_pattern=inverse_pattern, coupling=coupling, coupling_pattern=coupling_pattern, pivots=pivots, offsets=offsets, above_solution=above_solution)


def times_transposed(left_rows, matrix):
    return lax.dot_general(left_rows, matrix, (((1,), (1,)), ((), ())), preferred_element_type=jnp.float32)


def widen_pattern(pattern, block_size):
    return jnp.repeat(jnp.repeat(pattern, block_size, axis=0), block_size, axis=1)


def unit_inverse(raw_values, pattern):
    features = raw_values.shape[0]
    widened = widen_pattern(pattern, features // pattern.shape[0])
    row_ids = lax.broadcasted_iota(jnp.int32, (features, features), 0)
    col_ids = lax.broadcasted_iota(jnp.int32, (features, features), 1)
    kept_mask = (widened > 0) & (row_ids > col_ids)
    unit_part = jnp.where(row_ids == col_ids, jnp.ones_like(raw_values), jnp.zeros_like(raw_values))
    return jnp.where(kept_mask, raw_values, unit_part)


def masked_coupling(raw_values, pattern):
    widened = widen_pattern(pattern, raw_values.shape[0] // pattern.shape[0])
    return jnp.where(widened > 0, raw_values, jnp.zeros_like(raw_values))


def forward_node(packed):
    given, arriving, raw_values, pattern, link_raw, link_pattern, pivot_row = packed
    factor = unit_inverse(raw_values, pattern)
    linking = masked_coupling(link_raw, link_pattern)
    forward_rows = times_transposed((given - arriving).astype(jnp.bfloat16), factor)
    child_term = times_transposed(forward_rows.astype(jnp.bfloat16), linking).astype(jnp.bfloat16)
    return forward_rows * pivot_row[None, :], child_term


def backward_node(packed):
    weighted, parent_rows, raw_values, pattern, link_raw, link_pattern = packed
    factor = unit_inverse(raw_values, pattern)
    linking = masked_coupling(link_raw, link_pattern)
    reduced = weighted - jnp.dot(parent_rows, linking, preferred_element_type=jnp.float32)
    return jnp.dot(reduced.astype(jnp.bfloat16), factor, preferred_element_type=jnp.float32)


def reference(right_side, inverse_raw, inverse_pattern, coupling, coupling_pattern, pivots, offsets, above_solution):
    incoming = jnp.zeros(right_side.shape[1:], jnp.float32)
    kept_levels = []
    for level_index in range(LEVELS - 1, -1, -1):
        weighted, child_term = lax.map(forward_node, (right_side[level_index], incoming, inverse_raw[level_index], inverse_pattern[level_index], coupling[level_index], coupling_pattern[level_index], pivots[level_index]))
        kept_levels.insert(0, weighted)
        offset_row = offsets[level_index][:, None, None]
        terms_wide = child_term.astype(jnp.float32)
        own_terms = jnp.where(offset_row == 0, terms_wide, 0.0)
        moved_terms = jnp.where(offset_row == 1, terms_wide, 0.0)
        incoming = own_terms + jnp.concatenate([jnp.zeros_like(moved_terms[:1]), moved_terms[:-1]], axis=0)
    upper_rows = above_solution
    solutions = []
    for level_index in range(LEVELS):
        offset_row = offsets[level_index][:, None, None]
        next_upper = jnp.concatenate([upper_rows[1:], jnp.zeros_like(upper_rows[:1])], axis=0)
        parent_rows = jnp.where(offset_row == 1, next_upper, upper_rows)
        solved = lax.map(backward_node, (kept_levels[level_index], parent_rows, inverse_raw[level_index], inverse_pattern[level_index], coupling[level_index], coupling_pattern[level_index]))
        solutions.append(solved)
        upper_rows = solved.astype(jnp.bfloat16)
    return jnp.stack(solutions, axis=0)
```

```python
import functools

import jax
import jax.numpy as jnp
from jax import lax
from jax.experimental import pallas as pl
from jax.experimental.pallas import tpu as pltpu
from jax.sharding import PartitionSpec as P

ROWS = 32
BATCH = 128
TILE = 256
LANE = 128
AHEAD = 2
LAG = 7
LAG_STEP = 7
MESH = pl.DeviceIdType.MESH


def dot_nn(a, b):
    return lax.dot_general(a, b, (((1,), (0,)), ((), ())), preferred_element_type=jnp.float32)


def dot_nt(a, b):
    return lax.dot_general(a, b, (((1,), (1,)), ((), ())), preferred_element_type=jnp.float32)


def kernel(
    levels,
    nodes,
    rows,
    given_hbm,
    raw_hbm,
    pattern_ref,
    coupling_hbm,
    coupling_pattern_ref,
    pivot_ref,
    offsets_ref,
    above_hbm,
    out_ref,
    given,
    factor,
    link,
    gain,
    gain_t,
    inner,
    scaled_t,
    kept,
    red,
    up_out,
    up_own,
    up_side,
    dn_out,
    dn_own,
    dn_side,
    load_sems,
    up_sems,
    up_side_sems,
    dn_sems,
    dn_side_sems,
    above_sems,
):
    s = lax.axis_index("section")
    j = lax.axis_index("scen")
    total, features = given.shape
    pieces = total // rows
    batch = min(BATCH, total)
    blocks = pattern_ref.shape[0]
    size = features // blocks
    tile = min(TILE, features)
    tiles = range(0, features, tile)
    top, bottom = s == 0, s == levels - 1
    middle = jnp.logical_not(top | bottom)
    has_up, has_down = s > 0, s < levels - 1
    has_left, has_right = j > 0, j < nodes - 1
    up_id = {"section": lax.rem(s + levels - 1, levels)}
    down_id = {"section": lax.rem(s + 1, levels)}
    right_id = {"scen": lax.rem(j + 1, nodes)}
    left_id = {"scen": lax.rem(j + nodes - 1, nodes)}

    loads = [
        pltpu.make_async_copy(raw_hbm, factor, load_sems.at[0]),
        pltpu.make_async_copy(given_hbm, given, load_sems.at[1]),
        pltpu.make_async_copy(coupling_hbm, link, load_sems.at[2]),
    ]
    for load in loads:
        load.start()
    load_above = pltpu.make_async_copy(above_hbm, dn_own, load_sems.at[3])

    @pl.when(top)
    def _():
        load_above.start()

    barrier = pltpu.get_barrier_semaphore()
    count = jnp.int32(0)
    for has, where_to in ((has_up, up_id), (has_down, down_id), (has_left, left_id), (has_right, right_id)):

        @pl.when(has)
        def _(where_to=where_to):
            pl.semaphore_signal(barrier, inc=1, device_id=where_to, device_id_type=MESH)

        count = count + has.astype(jnp.int32)

    def piece(p):
        return pl.ds(pl.multiple_of(p * rows, rows), rows)

    def copy(src, dst, sems, p, device):
        return pltpu.make_async_remote_copy(
            src_ref=src.at[piece(p), :],
            dst_ref=dst.at[piece(p), :],
            send_sem=sems.at[0, p],
            recv_sem=sems.at[1, p],
            device_id=device,
            device_id_type=MESH,
        )

    def up_copy(p):
        return copy(up_out, up_own, up_sems, p, up_id)

    def up_relay(p):
        return copy(up_own, up_side, up_side_sems, p, right_id)

    def dn_copy(p):
        return copy(dn_out, dn_own, dn_sems, p, down_id)

    def dn_relay(p):
        return copy(dn_own, dn_side, dn_side_sems, p, left_id)

    def above_copy():
        return pltpu.make_async_remote_copy(
            src_ref=dn_own,
            dst_ref=dn_side,
            send_sem=above_sems.at[0],
            recv_sem=above_sems.at[1],
            device_id=left_id,
            device_id_type=MESH,
        )

    @pl.when(jnp.logical_not(has_left))
    def _():
        up_side[...] = jnp.zeros_like(up_side)

    @pl.when(jnp.logical_not(has_right))
    def _():
        dn_side[...] = jnp.zeros_like(dn_side)

    spread = (
        lax.broadcasted_iota(jnp.int32, (blocks, features), 1) // size
        == lax.broadcasted_iota(jnp.int32, (blocks, features), 0)
    ).astype(jnp.bfloat16)
    factor_mask = dot_nn(pattern_ref[...].astype(jnp.float32).astype(jnp.bfloat16), spread)
    link_mask = dot_nn(coupling_pattern_ref[...].astype(jnp.float32).astype(jnp.bfloat16), spread)
    loads[0].wait()
    for i in range(blocks):
        part = pl.ds(i * size, size)
        low = i * size // LANE * LANE
        high = (i * size // tile + 1) * tile
        if low > 0:
            mask = jnp.broadcast_to(factor_mask[i : i + 1, :low], (size, low)).astype(jnp.bfloat16)
            factor[part, :low] = factor[part, :low] * mask
        row_ids = lax.broadcasted_iota(jnp.int32, (size, LANE), 0) + i * size
        col_ids = lax.broadcasted_iota(jnp.int32, (size, LANE), 1) + low
        keep = (factor_mask[i : i + 1, low : low + LANE] > 0.5) & (row_ids > col_ids)
        unit = jnp.where(row_ids == col_ids, 1.0, 0.0)
        diagonal = factor[part, low : low + LANE].astype(jnp.float32)
        factor[part, low : low + LANE] = jnp.where(keep, diagonal, unit).astype(jnp.bfloat16)
        if high > low + LANE:
            factor[part, low + LANE : high] = jnp.zeros((size, high - low - LANE), jnp.bfloat16)
    loads[2].wait()
    for i in range(blocks):
        part = pl.ds(i * size, size)
        mask = jnp.broadcast_to(link_mask[i : i + 1, :], (size, features)).astype(jnp.bfloat16)
        link[part, :] = link[part, :] * mask
    loads[1].wait()
    pl.semaphore_wait(barrier, count)

    @pl.when(top)
    def _():
        load_above.wait()

        @pl.when(has_left)
        def _():
            above_copy().start()

    def big(b):
        return pl.ds(pl.multiple_of(b * batch, batch), batch)

    @pl.when(bottom)
    def _():
        def first(b, carry):
            here = big(b)
            given_rows = given[here, :].astype(jnp.bfloat16)
            forward = jnp.concatenate(
                [dot_nt(given_rows[:, : n + tile], factor[n : n + tile, : n + tile]) for n in tiles], axis=1
            )
            red[here, :] = (forward * pivot_ref[...]).astype(jnp.bfloat16)
            up_out[here, :] = dot_nt(forward.astype(jnp.bfloat16), link[...]).astype(jnp.bfloat16)
            for q in range(batch // rows):
                up_copy(b * (batch // rows) + q).start()
            return carry

        lax.fori_loop(0, total // batch, first, 0)

    for n in tiles:
        gain[:, n : n + tile] = dot_nn(link[:, n:], factor[n:, n : n + tile]).astype(jnp.bfloat16)

    @pl.when(middle)
    def _():
        for m in tiles:
            for n in tiles:
                gain_t[n : n + tile, m : m + tile] = gain[m : m + tile, n : n + tile].T

    @pl.when(has_down)
    def _():
        for m in tiles:
            for n in tiles:
                if m >= n:
                    turned = factor[m : m + tile, n : n + tile].T
                    scaled = turned.astype(jnp.float32) * pivot_ref[:, m : m + tile]
                    scaled_t[n : n + tile, m : m + tile] = scaled.astype(jnp.bfloat16)
        for m in tiles:
            for n in tiles:
                k = max(m, n)
                inner[m : m + tile, n : n + tile] = dot_nn(
                    scaled_t[m : m + tile, k:], factor[k:, n : n + tile]
                ).astype(jnp.bfloat16)

    @pl.when(bottom)
    def _():
        def own_part(b, carry):
            here = big(b)
            kept[here, :] = jnp.concatenate([dot_nn(red[here, n:], factor[n:, n : n + tile]) for n in tiles], axis=1)
            return carry

        lax.fori_loop(0, total // batch, own_part, 0)

    own_offset = offsets_ref[s, j]
    below = jnp.minimum(s + 1, levels - 1)
    from_own = (offsets_ref[below, j] == 0).astype(jnp.float32)
    from_side = (offsets_ref[below, jnp.maximum(j - 1, 0)] == 1).astype(jnp.float32)
    parent_own = (own_offset == 0).astype(jnp.float32)
    parent_side = (own_offset == 1).astype(jnp.float32)

    def parent_rows(here):
        return (
            dn_own[here, :].astype(jnp.float32) * parent_own + dn_side[here, :].astype(jnp.float32) * parent_side
        ).astype(jnp.bfloat16)

    def incoming_rows(here):
        return up_own[here, :].astype(jnp.float32) * from_own + up_side[here, :].astype(jnp.float32) * from_side

    @pl.when(top)
    def _():
        @pl.when(has_right)
        def _():
            above_copy().wait_recv()

        def own_part(b, carry):
            here = big(b)
            kept[here, :] = dot_nn(given[here, :].astype(jnp.bfloat16), inner[...]) - dot_nn(
                parent_rows(here), gain[...]
            )
            return carry

        lax.fori_loop(0, total // batch, own_part, 0)

    def forward_top(p):
        here = piece(p)
        result = kept[here, :] - dot_nn(incoming_rows(here).astype(jnp.bfloat16), inner[...])
        dn_out[here, :] = result.astype(jnp.bfloat16)
        dn_copy(p).start()
        out_ref[here, :] = result

    def forward(p):
        here = piece(p)
        reduced = (given[here, :] - incoming_rows(here)).astype(jnp.bfloat16)
        up_out[here, :] = dot_nn(reduced, gain_t[...]).astype(jnp.bfloat16)
        up_copy(p).start()
        red[here, :] = reduced

    def own_part(b):
        here = big(b)
        kept[here, :] = dot_nn(red[here, :], inner[...])

    def backward(p):
        here = piece(p)
        result = kept[here, :] - dot_nn(parent_rows(here), gain[...])

        @pl.when(has_down)
        def _():
            dn_out[here, :] = result.astype(jnp.bfloat16)
            dn_copy(p).start()

        out_ref[here, :] = result

    odd = lax.rem(j, 2)
    up_ahead = jnp.where((odd == 0) & has_left, AHEAD, 0)
    dn_ahead = jnp.where((odd == 1) & has_right, AHEAD, 0)
    lag = jnp.where(bottom, 0, LAG + LAG_STEP * (s - 1))
    group = batch // rows

    def within(p):
        return (p >= 0) & (p < pieces)

    def turn(u, carry):
        @pl.when(has_down & (u < pieces))
        def _():
            up_copy(u).wait_recv()

            @pl.when(has_right)
            def _():
                up_relay(u).start()

        f = u - up_ahead

        @pl.when(has_down & within(f))
        def _():
            @pl.when(has_left)
            def _():
                up_relay(f).wait_recv()

            @pl.when(top)
            def _():
                forward_top(f)

            @pl.when(middle)
            def _():
                forward(f)

        r = u - lag

        @pl.when(has_up & within(r))
        def _():
            dn_copy(r).wait_recv()

            @pl.when(has_left)
            def _():
                dn_relay(r).start()

        b = r - dn_ahead

        @pl.when(has_up & within(b))
        def _():
            @pl.when(has_right)
            def _():
                dn_relay(b).wait_recv()

            backward(b)

        @pl.when(middle & within(f) & (lax.rem(f, group) == group - 1))
        def _():
            own_part(lax.div(f, group))

        return carry

    turns = jnp.where(top, pieces + up_ahead, pieces + lag + dn_ahead)
    lax.fori_loop(0, turns, turn, 0)

    def finish(p, carry):
        @pl.when(has_up)
        def _():
            up_copy(p).wait_send()

            @pl.when(has_left)
            def _():
                dn_relay(p).wait_send()

        @pl.when(has_down)
        def _():
            dn_copy(p).wait_send()

            @pl.when(has_right)
            def _():
                up_relay(p).wait_send()

        return carry

    lax.fori_loop(0, pieces, finish, 0)

    @pl.when(top & has_left)
    def _():
        above_copy().wait_send()


def local(
    right_side,
    inverse_raw,
    inverse_pattern,
    coupling,
    coupling_pattern,
    pivots,
    offsets,
    above_solution,
):
    levels = lax.axis_size("section")
    nodes = lax.axis_size("scen")
    total, features = right_side.shape[2:]
    rows = min(ROWS, total)
    pieces = total // rows
    vmem = pl.BlockSpec(memory_space=pltpu.VMEM)
    hbm = pl.BlockSpec(memory_space=pl.ANY)
    half = pltpu.VMEM((total, features), jnp.bfloat16)
    whole = pltpu.VMEM((total, features), jnp.float32)
    square = pltpu.VMEM((features, features), jnp.bfloat16)
    sems = pltpu.SemaphoreType.DMA((2, pieces))
    solved = pl.pallas_call(
        functools.partial(kernel, levels, nodes, rows),
        out_shape=pltpu.VMEM((total, features), jnp.float32),
        in_specs=[hbm, hbm, vmem, hbm, vmem, vmem, pl.BlockSpec(memory_space=pltpu.SMEM), hbm],
        out_specs=vmem,
        scratch_shapes=[whole]
        + [square] * 6
        + [whole]
        + [half] * 7
        + [pltpu.SemaphoreType.DMA((4,))]
        + [sems] * 4
        + [pltpu.SemaphoreType.DMA((2,))],
        compiler_params=pltpu.CompilerParams(
            collective_id=0, has_side_effects=True, vmem_limit_bytes=60 * 1024 * 1024
        ),
    )(
        right_side[0, 0],
        inverse_raw[0, 0],
        inverse_pattern[0, 0],
        coupling[0, 0],
        coupling_pattern[0, 0],
        pivots[0],
        offsets,
        above_solution[0],
    )
    return solved[None, None]


def solution(mesh):
    placed = (
        P("section", "scen", None, None),
        P("section", "scen", None, None),
        P("section", "scen", None, None),
        P("section", "scen", None, None),
        P("section", "scen", None, None),
        P("section", "scen", None),
        P(),
        P("scen", None, None),
    )
    return jax.shard_map(
        local,
        mesh=mesh,
        in_specs=placed,
        out_specs=P("section", "scen", None, None),
        check_vma=False,
    )
```

```python
import functools

import jax
import jax.numpy as jnp
from jax import lax
from jax.experimental import pallas as pl
from jax.experimental.pallas import tpu as pltpu
from jax.sharding import PartitionSpec as P

ROWS = 32
SMALL = 16
COUNT = 0
BATCH = 128
TILE = 256
LANE = 128
ROUTES = ((1, 2, 0, 256),)
MESH = pl.DeviceIdType.MESH


def dot_nn(a, b):
    return lax.dot_general(a, b, (((1,), (0,)), ((), ())), preferred_element_type=jnp.float32)


def dot_nt(a, b):
    return lax.dot_general(a, b, (((1,), (1,)), ((), ())), preferred_element_type=jnp.float32)


RELAY_UP, RELAY_DOWN, FORWARD, BACKWARD, OWN, PASS_UP, PASS_DOWN = range(7)
KINDS = 8
DIGITS = 10


def piece_rows(total):
    count = COUNT if total >= COUNT * SMALL + ROWS else 0
    sizes = [SMALL] * count + [min(ROWS, total)] * ((total - count * SMALL) // min(ROWS, total))
    starts = [sum(sizes[:p]) for p in range(len(sizes))]
    return count, sizes, starts


def routed_piece(a, b, start):
    return any((a, b) == (src, dst) and low <= start < high for src, dst, low, high in ROUTES)


def orders(levels, sizes, starts, batch):
    pieces = len(sizes)
    wire = [0.022 * size for size in sizes]
    far, near, work = 2.25, 1.1, 0.6
    steps = {(s, o): [] for s in range(levels) for o in (0, 1)}
    group = [start // batch for start in starts]

    def hop(a, b, time, o, p):
        time += far + 2 * wire[p]
        if routed_piece(a, b, starts[p]):
            steps[(a + levels // 2) % levels, o].append((time, 0, PASS_UP if b < a else PASS_DOWN, p))
            time += far + 2 * wire[p]
        return time + (0.5 if {a, b} == {1, 2} else 0.0)

    def stage(s, src, kind, relay, sent):
        own = [[hop(src, s, sent[o][p], o, p) for p in range(pieces)] for o in (0, 1)]
        done = [[], []]
        for o in (0, 1):
            close = (o == 1) == (relay == RELAY_UP)
            before = arrived = 0.0
            for p in range(pieces):
                arrived = max(arrived, own[o][p])
                steps[s, o].append((arrived, 1, relay, p))
                time = max(arrived, own[1 - o][p] + (near if close else far + wire[p]), before)
                steps[s, o].append((time, 2, kind, p))
                before = time + work
                done[o].append(before)
        return done

    sent = [[4.0 + 0.0444 * start for start in starts]] * 2
    for s in range(levels - 2, -1, -1):
        sent = stage(s, s + 1, FORWARD, RELAY_UP, sent)
        if s > 0:
            for o in (0, 1):
                for g in range(group[-1] + 1):
                    end = max(sent[o][p] for p in range(pieces) if group[p] == g)
                    steps[s, o].append((end + 0.5, 3, OWN, g))
    for s in range(1, levels):
        sent = stage(s, s - 1, BACKWARD, RELAY_DOWN, sent)
    ordered = {}
    for key, listed in steps.items():
        rows_done, taken = set(), []
        for _, _, kind, p in sorted(listed):
            if kind == BACKWARD and key[0] < levels - 1 and group[p] not in rows_done:
                rows_done.add(group[p])
                taken.append(OWN)
            if kind == OWN:
                if p in rows_done:
                    continue
                rows_done.add(p)
            taken.append(kind)
        ordered[key] = taken
    return ordered


def kernel(
    levels,
    nodes,
    given_hbm,
    raw_hbm,
    pattern_ref,
    coupling_hbm,
    coupling_pattern_ref,
    pivot_ref,
    offsets_ref,
    above_hbm,
    out_ref,
    given,
    factor,
    link,
    gain,
    gain_t,
    inner,
    scaled_t,
    kept,
    red,
    up_out,
    up_own,
    up_side,
    dn_out,
    dn_own,
    dn_side,
    up_pass,
    dn_pass,
    load_sems,
    up_sems,
    up_side_sems,
    dn_sems,
    dn_side_sems,
    up_pass_sems,
    dn_pass_sems,
    above_sems,
):
    s = lax.axis_index("section")
    j = lax.axis_index("scen")
    total, features = given.shape
    count, sizes, starts = piece_rows(total)
    pieces = len(sizes)
    batch = min(BATCH, total)
    blocks = pattern_ref.shape[0]
    size = features // blocks
    tile = min(TILE, features)
    tiles = range(0, features, tile)
    top, bottom = s == 0, s == levels - 1
    middle = jnp.logical_not(top | bottom)
    has_up, has_down = s > 0, s < levels - 1
    has_left, has_right = j > 0, j < nodes - 1
    up_id = {"section": lax.rem(s + levels - 1, levels)}
    down_id = {"section": lax.rem(s + 1, levels)}
    right_id = {"scen": lax.rem(j + 1, nodes)}
    left_id = {"scen": lax.rem(j + nodes - 1, nodes)}

    loads = [
        pltpu.make_async_copy(raw_hbm, factor, load_sems.at[0]),
        pltpu.make_async_copy(given_hbm, given, load_sems.at[1]),
        pltpu.make_async_copy(coupling_hbm, link, load_sems.at[2]),
    ]
    for load in loads:
        load.start()
    load_above = pltpu.make_async_copy(above_hbm, dn_own, load_sems.at[3])

    @pl.when(top)
    def _():
        load_above.start()

    barrier = pltpu.get_barrier_semaphore()
    for step in range(1, levels):
        pl.semaphore_signal(
            barrier, inc=1, device_id={"section": lax.rem(s + step, levels)}, device_id_type=MESH
        )
    for has, where_to in ((has_left, left_id), (has_right, right_id)):

        @pl.when(has)
        def _(where_to=where_to):
            pl.semaphore_signal(barrier, inc=1, device_id=where_to, device_id_type=MESH)

    greeted = levels - 1 + has_left.astype(jnp.int32) + has_right.astype(jnp.int32)

    def sized(p, act):
        if isinstance(p, int):
            act(p, pl.ds(starts[p], sizes[p]))
            return
        rows = sizes[-1]
        if count:

            @pl.when(p < count)
            def _():
                act(p, pl.ds(pl.multiple_of(p * SMALL, SMALL), SMALL))

            @pl.when(p >= count)
            def _():
                act(p, pl.ds(pl.multiple_of(count * SMALL + (p - count) * rows, SMALL), rows))

        else:
            act(p, pl.ds(pl.multiple_of(p * rows, rows), rows))

    def copy(src, dst, send_sem, recv_sem, here, device):
        return pltpu.make_async_remote_copy(
            src_ref=src.at[here, :],
            dst_ref=dst.at[here, :],
            send_sem=send_sem,
            recv_sem=recv_sem,
            device_id=device,
            device_id_type=MESH,
        )

    def up_copy(p, here):
        return copy(up_out, up_own, up_sems.at[0, p], up_sems.at[1, p], here, up_id)

    def up_relay(p, here):
        return copy(up_own, up_side, up_side_sems.at[0, p], up_side_sems.at[1, p], here, right_id)

    def dn_copy(p, here):
        return copy(dn_out, dn_own, dn_sems.at[0, p], dn_sems.at[1, p], here, down_id)

    def dn_relay(p, here):
        return copy(dn_own, dn_side, dn_side_sems.at[0, p], dn_side_sems.at[1, p], here, left_id)

    middle_id = {"section": lax.rem(s + levels // 2, levels)}
    origin = lax.rem(s + levels // 2, levels)

    def up_detour(p, here):
        return copy(up_out, up_pass, up_sems.at[0, p], up_pass_sems.at[1, p], here, middle_id)

    def up_on(p, here):
        device = {"section": lax.rem(origin + levels - 1, levels)}
        return copy(up_pass, up_own, up_pass_sems.at[0, p], up_sems.at[1, p], here, device)

    def dn_detour(p, here):
        return copy(dn_out, dn_pass, dn_sems.at[0, p], dn_pass_sems.at[1, p], here, middle_id)

    def dn_on(p, here):
        device = {"section": lax.rem(origin + 1, levels)}
        return copy(dn_pass, dn_own, dn_pass_sems.at[0, p], dn_sems.at[1, p], here, device)

    def row_of(p):
        return p * SMALL if count == 0 and sizes[-1] == SMALL else jnp.where(
            p < count, p * SMALL, count * SMALL + (p - count) * sizes[-1]
        )

    def routed(a, upward, p):
        found = jnp.bool_(False)
        start = row_of(p)
        for src, dst, low, high in ROUTES:
            if (dst < src) == upward:
                found = found | ((a == src) & (start >= low) & (start < high))
        return found

    def send(p, here, upward):
        straight, detour = (up_copy, up_detour) if upward else (dn_copy, dn_detour)
        if not any((dst < src) == upward for src, dst, _, _ in ROUTES):
            straight(p, here).start()
            return
        round_about = routed(s, upward, p)

        @pl.when(round_about)
        def _():
            detour(p, here).start()

        @pl.when(jnp.logical_not(round_about))
        def _():
            straight(p, here).start()

    odd = lax.rem(j, 2)
    listed = orders(levels, sizes, starts, batch)
    turns = jnp.int32(0)
    words = [jnp.int32(0)] * -(-max(len(steps) for steps in listed.values()) // DIGITS)
    for (section, parity), steps in listed.items():
        mine = (s == section) & (odd == parity)
        turns = jnp.where(mine, len(steps), turns)
        for w in range(len(words)):
            digits = steps[w * DIGITS : (w + 1) * DIGITS]
            packed = sum(kind * KINDS**i for i, kind in enumerate(digits))
            words[w] = jnp.where(mine, packed, words[w])

    def first_routed(upward):
        found = jnp.int32(0)
        for src, dst, low, high in ROUTES:
            if (dst < src) == upward:
                p = sum(start < low for start in starts)
                found = jnp.where(lax.rem(src + levels // 2, levels) == s, p, found)
        return found

    def above_copy():
        return pltpu.make_async_remote_copy(
            src_ref=dn_own,
            dst_ref=dn_side,
            send_sem=above_sems.at[0],
            recv_sem=above_sems.at[1],
            device_id=left_id,
            device_id_type=MESH,
        )

    @pl.when(jnp.logical_not(has_left))
    def _():
        up_side[...] = jnp.zeros_like(up_side)

    @pl.when(jnp.logical_not(has_right))
    def _():
        dn_side[...] = jnp.zeros_like(dn_side)

    spread = (
        lax.broadcasted_iota(jnp.int32, (blocks, features), 1) // size
        == lax.broadcasted_iota(jnp.int32, (blocks, features), 0)
    ).astype(jnp.bfloat16)
    factor_mask = dot_nn(pattern_ref[...].astype(jnp.float32).astype(jnp.bfloat16), spread)
    link_mask = dot_nn(coupling_pattern_ref[...].astype(jnp.float32).astype(jnp.bfloat16), spread)
    loads[0].wait()
    for i in range(blocks):
        part = pl.ds(i * size, size)
        low = i * size // LANE * LANE
        high = (i * size // tile + 1) * tile
        if low > 0:
            mask = jnp.broadcast_to(factor_mask[i : i + 1, :low], (size, low)).astype(jnp.bfloat16)
            factor[part, :low] = factor[part, :low] * mask
        row_ids = lax.broadcasted_iota(jnp.int32, (size, LANE), 0) + i * size
        col_ids = lax.broadcasted_iota(jnp.int32, (size, LANE), 1) + low
        keep = (factor_mask[i : i + 1, low : low + LANE] > 0.5) & (row_ids > col_ids)
        unit = jnp.where(row_ids == col_ids, 1.0, 0.0)
        diagonal = factor[part, low : low + LANE].astype(jnp.float32)
        factor[part, low : low + LANE] = jnp.where(keep, diagonal, unit).astype(jnp.bfloat16)
        if high > low + LANE:
            factor[part, low + LANE : high] = jnp.zeros((size, high - low - LANE), jnp.bfloat16)
    loads[2].wait()
    for i in range(blocks):
        part = pl.ds(i * size, size)
        mask = jnp.broadcast_to(link_mask[i : i + 1, :], (size, features)).astype(jnp.bfloat16)
        link[part, :] = link[part, :] * mask
    loads[1].wait()
    pl.semaphore_wait(barrier, greeted)

    @pl.when(top)
    def _():
        load_above.wait()

        @pl.when(has_left)
        def _():
            above_copy().start()

    def big(b):
        return pl.ds(pl.multiple_of(b * batch, batch), batch)

    def first_terms(here):
        given_rows = given[here, :].astype(jnp.bfloat16)
        forward = jnp.concatenate(
            [dot_nt(given_rows[:, : n + tile], factor[n : n + tile, : n + tile]) for n in tiles], axis=1
        )
        red[here, :] = (forward * pivot_ref[...]).astype(jnp.bfloat16)
        up_out[here, :] = dot_nt(forward.astype(jnp.bfloat16), link[...]).astype(jnp.bfloat16)

    @pl.when(bottom)
    def _():
        begin = 0
        for end in (sizes[-1], batch):
            if end > begin:
                first_terms(pl.ds(begin, end - begin))
                for p in range(pieces):
                    if begin <= starts[p] < end:
                        sized(p, lambda p, here: send(p, here, True))
            begin = end
        head = sum(start < batch for start in starts)
        per_batch = batch // sizes[-1]

        def first(b, carry):
            first_terms(big(b))
            for q in range(per_batch):
                p = head + (b - 1) * per_batch + q
                here = pl.ds(pl.multiple_of(b * batch + q * sizes[-1], sizes[-1]), sizes[-1])
                send(p, here, True)
            return carry

        lax.fori_loop(1, total // batch, first, 0)

    for n in tiles:
        gain[:, n : n + tile] = dot_nn(link[:, n:], factor[n:, n : n + tile]).astype(jnp.bfloat16)

    @pl.when(middle)
    def _():
        for m in tiles:
            for n in tiles:
                gain_t[n : n + tile, m : m + tile] = gain[m : m + tile, n : n + tile].T

    @pl.when(has_down)
    def _():
        for m in tiles:
            for n in tiles:
                if m >= n:
                    turned = factor[m : m + tile, n : n + tile].T
                    scaled = turned.astype(jnp.float32) * pivot_ref[:, m : m + tile]
                    scaled_t[n : n + tile, m : m + tile] = scaled.astype(jnp.bfloat16)
        for m in tiles:
            for n in tiles:
                k = max(m, n)
                inner[m : m + tile, n : n + tile] = dot_nn(
                    scaled_t[m : m + tile, k:], factor[k:, n : n + tile]
                ).astype(jnp.bfloat16)

    @pl.when(bottom)
    def _():
        def own_part(b, carry):
            here = big(b)
            kept[here, :] = jnp.concatenate([dot_nn(red[here, n:], factor[n:, n : n + tile]) for n in tiles], axis=1)
            return carry

        lax.fori_loop(0, total // batch, own_part, 0)

    own_offset = offsets_ref[s, j]
    below = jnp.minimum(s + 1, levels - 1)
    from_own = (offsets_ref[below, j] == 0).astype(jnp.float32)
    from_side = (offsets_ref[below, jnp.maximum(j - 1, 0)] == 1).astype(jnp.float32)
    parent_own = (own_offset == 0).astype(jnp.float32)
    parent_side = (own_offset == 1).astype(jnp.float32)

    def parent_rows(here):
        return (
            dn_own[here, :].astype(jnp.float32) * parent_own + dn_side[here, :].astype(jnp.float32) * parent_side
        ).astype(jnp.bfloat16)

    def incoming_rows(here):
        return up_own[here, :].astype(jnp.float32) * from_own + up_side[here, :].astype(jnp.float32) * from_side

    @pl.when(top)
    def _():
        @pl.when(has_right)
        def _():
            above_copy().wait_recv()

        def own_part(b, carry):
            here = big(b)
            kept[here, :] = dot_nn(given[here, :].astype(jnp.bfloat16), inner[...]) - dot_nn(
                parent_rows(here), gain[...]
            )
            return carry

        lax.fori_loop(0, total // batch, own_part, 0)

    def forward_top(p, here):
        result = kept[here, :] - dot_nn(incoming_rows(here).astype(jnp.bfloat16), inner[...])
        dn_out[here, :] = result.astype(jnp.bfloat16)
        send(p, here, False)
        out_ref[here, :] = result

    def forward(p, here):
        reduced = (given[here, :] - incoming_rows(here)).astype(jnp.bfloat16)
        up_out[here, :] = dot_nn(reduced, gain_t[...]).astype(jnp.bfloat16)
        send(p, here, True)
        red[here, :] = reduced

    def backward(p, here):
        result = kept[here, :] - dot_nn(parent_rows(here), gain[...])

        @pl.when(has_down)
        def _():
            dn_out[here, :] = result.astype(jnp.bfloat16)
            send(p, here, False)

        out_ref[here, :] = result

    def relay_up(p, here):
        up_copy(p, here).wait_recv()

        @pl.when(has_right)
        def _():
            up_relay(p, here).start()

    def relay_down(p, here):
        dn_copy(p, here).wait_recv()

        @pl.when(has_left)
        def _():
            dn_relay(p, here).start()

    def forward_any(p, here):
        @pl.when(has_left)
        def _():
            up_relay(p, here).wait_recv()

        @pl.when(top)
        def _():
            forward_top(p, here)

        @pl.when(middle)
        def _():
            forward(p, here)

    def backward_any(p, here):
        @pl.when(has_right)
        def _():
            dn_relay(p, here).wait_recv()

        backward(p, here)

    def pass_up(p, here):
        up_detour(p, here).wait_recv()
        up_on(p, here).start()

    def pass_down(p, here):
        dn_detour(p, here).wait_recv()
        dn_on(p, here).start()

    acts = {RELAY_UP: relay_up, RELAY_DOWN: relay_down, FORWARD: forward_any, BACKWARD: backward_any}
    if any(dst < src for src, dst, _, _ in ROUTES):
        acts[PASS_UP] = pass_up
    if any(dst > src for src, dst, _, _ in ROUTES):
        acts[PASS_DOWN] = pass_down

    def turn(i, carry):
        word, counts = carry
        block = lax.div(i, DIGITS)
        fresh = words[0]
        for w in range(1, len(words)):
            fresh = jnp.where(block == w, words[w], fresh)
        word = jnp.where(lax.rem(i, DIGITS) == 0, fresh, word)
        kind = lax.rem(word, KINDS)
        p = counts[0]
        for which in range(1, len(counts)):
            p = jnp.where(kind == which, counts[which], p)
        for which, act in acts.items():

            @pl.when(kind == which)
            def _(act=act):
                sized(p, act)

        @pl.when(kind == OWN)
        def _():
            here = big(p)
            kept[here, :] = dot_nn(red[here, :], inner[...])

        counts = tuple(jnp.where(kind == which, c + 1, c) for which, c in enumerate(counts))
        return lax.div(word, KINDS), counts

    counts = [jnp.int32(0)] * (KINDS - 1)
    counts[PASS_UP], counts[PASS_DOWN] = first_routed(True), first_routed(False)
    lax.fori_loop(0, turns, turn, (jnp.int32(0), tuple(counts)))

    def drain(p, here):
        @pl.when(has_up)
        def _():
            up_copy(p, here).wait_send()

            @pl.when(has_left)
            def _():
                dn_relay(p, here).wait_send()

        @pl.when(has_down)
        def _():
            dn_copy(p, here).wait_send()

            @pl.when(has_right)
            def _():
                up_relay(p, here).wait_send()

        if PASS_UP in acts:

            @pl.when(routed(origin, True, p))
            def _():
                up_on(p, here).wait_send()

        if PASS_DOWN in acts:

            @pl.when(routed(origin, False, p))
            def _():
                dn_on(p, here).wait_send()

    def finish(p, carry):
        sized(p, drain)
        return carry

    lax.fori_loop(0, pieces, finish, 0)

    @pl.when(top & has_left)
    def _():
        above_copy().wait_send()


def local(
    right_side,
    inverse_raw,
    inverse_pattern,
    coupling,
    coupling_pattern,
    pivots,
    offsets,
    above_solution,
):
    levels = lax.axis_size("section")
    nodes = lax.axis_size("scen")
    total, features = right_side.shape[2:]
    _, sizes, starts = piece_rows(total)
    pieces = len(sizes)
    vmem = pl.BlockSpec(memory_space=pltpu.VMEM)
    hbm = pl.BlockSpec(memory_space=pl.ANY)
    half = pltpu.VMEM((total, features), jnp.bfloat16)
    whole = pltpu.VMEM((total, features), jnp.float32)
    square = pltpu.VMEM((features, features), jnp.bfloat16)
    sems = pltpu.SemaphoreType.DMA((2, pieces))
    solved = pl.pallas_call(
        functools.partial(kernel, levels, nodes),
        out_shape=pltpu.VMEM((total, features), jnp.float32),
        in_specs=[hbm, hbm, vmem, hbm, vmem, vmem, pl.BlockSpec(memory_space=pltpu.SMEM), hbm],
        out_specs=vmem,
        scratch_shapes=[whole]
        + [square] * 6
        + [whole]
        + [half] * 9
        + [pltpu.SemaphoreType.DMA((4,))]
        + [sems] * 6
        + [pltpu.SemaphoreType.DMA((2,))],
        compiler_params=pltpu.CompilerParams(
            collective_id=0, has_side_effects=True, vmem_limit_bytes=60 * 1024 * 1024
        ),
    )(
        right_side[0, 0],
        inverse_raw[0, 0],
        inverse_pattern[0, 0],
        coupling[0, 0],
        coupling_pattern[0, 0],
        pivots[0],
        offsets,
        above_solution[0],
    )
    return solved[None, None]


def solution(mesh):
    placed = (
        P("section", "scen", None, None),
        P("section", "scen", None, None),
        P("section", "scen", None, None),
        P("section", "scen", None, None),
        P("section", "scen", None, None),
        P("section", "scen", None),
        P(),
        P("scen", None, None),
    )
    return jax.shard_map(
        local,
        mesh=mesh,
        in_specs=placed,
        out_specs=P("section", "scen", None, None),
        check_vma=False,
    )
```

```python
import functools

import jax
import jax.numpy as jnp
from jax import lax
from jax.experimental import pallas as pl
from jax.experimental.pallas import tpu as pltpu
from jax.sharding import PartitionSpec as P

ROWS = 32
CHUNKS = 1
BATCH = 128
TILE = 256
LANE = 128
ROUTES = ((1, 2, 0, 256), (2, 3, 288, 320))
MESH = pl.DeviceIdType.MESH


def dot_nn(a, b):
    return lax.dot_general(a, b, (((1,), (0,)), ((), ())), preferred_element_type=jnp.float32)


def dot_nt(a, b):
    return lax.dot_general(a, b, (((1,), (1,)), ((), ())), preferred_element_type=jnp.float32)


RELAY_UP, RELAY_DOWN, FORWARD, BACKWARD, OWN, PASS_UP, PASS_DOWN = range(7)
KINDS = 8
DIGITS = 10


ACROSS, CORNER, FAR, NEAR, WORK, EVERY, FIRST, DETOUR, LATER, CHUNK = (4.03, 0.39, 3.47, 1.27, 0.89, 1.68, 3.24, 2.84, 0.23, 0.0)


def routed_piece(a, b, start):
    return any((a, b) == (src, dst) and low <= start < high for src, dst, low, high in ROUTES)


def orders(levels, pieces, rows, batch):
    steps = {(s, o): [] for s in range(levels) for o in (0, 1)}
    chunks = range(CHUNKS)
    group = batch // rows

    def hop(a, b, time, o, p, q):
        if routed_piece(a, b, p * rows):
            kind = PASS_UP if b < a else PASS_DOWN
            steps[(a + levels // 2) % levels, o].append((time + ACROSS, 0, kind, p * CHUNKS + q))
            time += DETOUR
        return time + ACROSS + (CORNER if {a, b} == {1, 2} else 0.0)

    def stage(s, src, kind, relay, sent):
        own = [[[hop(src, s, sent[o][p][q], o, p, q) for q in chunks] for p in range(pieces)] for o in (0, 1)]
        done = [[], []]
        for o in (0, 1):
            side = NEAR if (o == 1) == (relay == RELAY_UP) else FAR
            before = arrived = 0.0
            for p in range(pieces):
                for q in chunks:
                    arrived = max(arrived, own[o][p][q])
                    steps[s, o].append((arrived, 1, relay, p * CHUNKS + q))
                early = max(own[o][p][0], own[1 - o][p][0] + side, before)
                time = max(arrived, own[1 - o][p][-1] + side, before)
                if CHUNKS > 1:
                    time = max(time - WORK / CHUNKS, early)
                steps[s, o].append((time, 2, kind, p))
                before = time + WORK
                done[o].append([time + WORK * (0.75 + 0.25 * q if CHUNKS > 1 else 1.0) for q in chunks])
        return done

    sent = [[[FIRST + EVERY * p + CHUNK * q for q in chunks] for p in range(pieces)]] * 2
    for s in range(levels - 2, -1, -1):
        sent = stage(s, s + 1, FORWARD, RELAY_UP, sent)
        if s > 0:
            for o in (0, 1):
                for g in range(pieces // group):
                    steps[s, o].append((sent[o][(g + 1) * group - 1][-1] + LATER, 3, OWN, g))
    for s in range(1, levels):
        sent = stage(s, s - 1, BACKWARD, RELAY_DOWN, sent)
    ordered = {}
    for key, listed in steps.items():
        parts_done, taken = set(), []
        for _, _, kind, p in sorted(listed):
            if kind == BACKWARD and key[0] < levels - 1 and p // group not in parts_done:
                parts_done.add(p // group)
                taken.append(OWN)
            if kind == OWN:
                if p in parts_done:
                    continue
                parts_done.add(p)
            taken.append(kind)
        ordered[key] = taken
    return ordered


def kernel(
    levels,
    nodes,
    given_hbm,
    raw_hbm,
    pattern_hbm,
    coupling_hbm,
    coupling_pattern_hbm,
    pivot_hbm,
    offsets_hbm,
    above_hbm,
    out_ref,
    given,
    factor,
    link,
    gain,
    gain_t,
    inner,
    scaled_t,
    kept,
    red,
    up_out,
    up_own,
    up_side,
    dn_out,
    dn_own,
    dn_side,
    up_pass,
    dn_pass,
    pattern_ref,
    coupling_pattern_ref,
    pivot_ref,
    offsets_ref,
    load_sems,
    up_sems,
    up_side_sems,
    dn_sems,
    dn_side_sems,
    up_pass_sems,
    dn_pass_sems,
    above_sems,
):
    s = lax.axis_index("section")
    j = lax.axis_index("scen")
    total, features = given.shape
    rows = min(ROWS, total)
    pieces = total // rows
    batch = min(BATCH, total)
    chunk = features // CHUNKS
    spans = [slice(q * chunk, (q + 1) * chunk) for q in range(CHUNKS)]
    blocks = pattern_ref.shape[0]
    size = features // blocks
    tile = min(TILE, features)
    tiles = range(0, features, tile)
    top, bottom = s == 0, s == levels - 1
    middle = jnp.logical_not(top | bottom)
    has_up, has_down = s > 0, s < levels - 1
    has_left, has_right = j > 0, j < nodes - 1
    up_id = {"section": lax.rem(s + levels - 1, levels)}
    down_id = {"section": lax.rem(s + 1, levels)}
    right_id = {"scen": lax.rem(j + 1, nodes)}
    left_id = {"scen": lax.rem(j + nodes - 1, nodes)}

    loads = [
        pltpu.make_async_copy(raw_hbm, factor, load_sems.at[0]),
        pltpu.make_async_copy(given_hbm, given, load_sems.at[1]),
        pltpu.make_async_copy(coupling_hbm, link, load_sems.at[2]),
    ]
    small_loads = [
        pltpu.make_async_copy(src, dst, load_sems.at[4 + i])
        for i, (src, dst) in enumerate(
            (
                (pattern_hbm, pattern_ref),
                (coupling_pattern_hbm, coupling_pattern_ref),
                (pivot_hbm, pivot_ref),
                (offsets_hbm, offsets_ref),
            )
        )
    ]
    above_loads = [
        pltpu.make_async_copy(above_hbm.at[:, span], dn_own.at[q], above_sems.at[2 + q])
        for q, span in enumerate(spans)
    ]

    barrier = pltpu.get_barrier_semaphore()
    for step in range(1, levels):
        pl.semaphore_signal(
            barrier, inc=1, device_id={"section": lax.rem(s + step, levels)}, device_id_type=MESH
        )
    for has, where_to in ((has_left, left_id), (has_right, right_id)):

        @pl.when(has)
        def _(where_to=where_to):
            pl.semaphore_signal(barrier, inc=1, device_id=where_to, device_id_type=MESH)

    for load in small_loads + loads:
        load.start()

    @pl.when(top)
    def _():
        for load in above_loads:
            load.start()

    greeted = levels - 1 + has_left.astype(jnp.int32) + has_right.astype(jnp.int32)

    def piece(p):
        return pl.ds(pl.multiple_of(p * rows, rows), rows)

    def copy(src, dst, send_sems, recv_sems, m, device):
        p, q = lax.div(m, CHUNKS), lax.rem(m, CHUNKS)
        return pltpu.make_async_remote_copy(
            src_ref=src.at[q, piece(p), :],
            dst_ref=dst.at[q, piece(p), :],
            send_sem=send_sems.at[0, m],
            recv_sem=recv_sems.at[1, m],
            device_id=device,
            device_id_type=MESH,
        )

    def up_copy(m):
        return copy(up_out, up_own, up_sems, up_sems, m, up_id)

    def up_relay(m):
        return copy(up_own, up_side, up_side_sems, up_side_sems, m, right_id)

    def dn_copy(m):
        return copy(dn_out, dn_own, dn_sems, dn_sems, m, down_id)

    def dn_relay(m):
        return copy(dn_own, dn_side, dn_side_sems, dn_side_sems, m, left_id)

    def above_copy():
        return pltpu.make_async_remote_copy(
            src_ref=dn_own,
            dst_ref=dn_side,
            send_sem=above_sems.at[0],
            recv_sem=above_sems.at[1],
            device_id=left_id,
            device_id_type=MESH,
        )

    middle_id = {"section": lax.rem(s + levels // 2, levels)}
    origin = lax.rem(s + levels // 2, levels)

    def up_detour(m):
        return copy(up_out, up_pass, up_sems, up_pass_sems, m, middle_id)

    def up_on(m):
        device = {"section": lax.rem(origin + levels - 1, levels)}
        return copy(up_pass, up_own, up_pass_sems, up_sems, m, device)

    def dn_detour(m):
        return copy(dn_out, dn_pass, dn_sems, dn_pass_sems, m, middle_id)

    def dn_on(m):
        device = {"section": lax.rem(origin + 1, levels)}
        return copy(dn_pass, dn_own, dn_pass_sems, dn_sems, m, device)

    def routed(a, upward, p):
        found = jnp.bool_(False)
        for src, dst, low, high in ROUTES:
            if (dst < src) == upward:
                found = found | ((a == src) & (p >= low // rows) & (p < high // rows))
        return found

    def send(p, q, upward):
        m = p * CHUNKS + q
        straight, detour = (up_copy, up_detour) if upward else (dn_copy, dn_detour)
        if not any((dst < src) == upward for src, dst, _, _ in ROUTES):
            straight(m).start()
            return
        round_about = routed(s, upward, p)

        @pl.when(round_about)
        def _():
            detour(m).start()

        @pl.when(jnp.logical_not(round_about))
        def _():
            straight(m).start()

    odd = lax.rem(j, 2)
    listed = orders(levels, pieces, rows, batch)
    turns = jnp.int32(0)
    words = [jnp.int32(0)] * -(-max(len(steps) for steps in listed.values()) // DIGITS)
    for (section, parity), steps in listed.items():
        mine = (s == section) & (odd == parity)
        turns = jnp.where(mine, len(steps), turns)
        for w in range(len(words)):
            digits = steps[w * DIGITS : (w + 1) * DIGITS]
            packed = sum(kind * KINDS**i for i, kind in enumerate(digits))
            words[w] = jnp.where(mine, packed, words[w])

    def routed_messages(upward):
        found = {}
        for src, dst, low, high in sorted(ROUTES):
            if (dst < src) == upward:
                found.setdefault(src, []).append((low // rows * CHUNKS, high // rows * CHUNKS))
        return found

    def routed_message(upward, n):
        m = n
        for src, spans_of in routed_messages(upward).items():
            skipped, total_of, last = 0, 0, 0
            for low, high in spans_of:
                skipped += low - last
                m = jnp.where((origin == src) & (n >= total_of), n + skipped, m)
                total_of += high - low
                last = high
        return m

    @pl.when(jnp.logical_not(has_left))
    def _():
        up_side[...] = jnp.zeros_like(up_side)

    @pl.when(jnp.logical_not(has_right))
    def _():
        dn_side[...] = jnp.zeros_like(dn_side)

    spread = (
        lax.broadcasted_iota(jnp.int32, (blocks, features), 1) // size
        == lax.broadcasted_iota(jnp.int32, (blocks, features), 0)
    ).astype(jnp.bfloat16)
    for load in small_loads:
        load.wait()
    factor_mask = dot_nn(pattern_ref[...].astype(jnp.float32).astype(jnp.bfloat16), spread)
    link_mask = dot_nn(coupling_pattern_ref[...].astype(jnp.float32).astype(jnp.bfloat16), spread)
    loads[0].wait()
    for i in range(blocks):
        part = pl.ds(i * size, size)
        low = i * size // LANE * LANE
        high = (i * size // tile + 1) * tile
        if low > 0:
            mask = jnp.broadcast_to(factor_mask[i : i + 1, :low], (size, low)).astype(jnp.bfloat16)
            factor[part, :low] = factor[part, :low] * mask
        row_ids = lax.broadcasted_iota(jnp.int32, (size, LANE), 0) + i * size
        col_ids = lax.broadcasted_iota(jnp.int32, (size, LANE), 1) + low
        keep = (factor_mask[i : i + 1, low : low + LANE] > 0.5) & (row_ids > col_ids)
        unit = jnp.where(row_ids == col_ids, 1.0, 0.0)
        diagonal = factor[part, low : low + LANE].astype(jnp.float32)
        factor[part, low : low + LANE] = jnp.where(keep, diagonal, unit).astype(jnp.bfloat16)
        if high > low + LANE:
            factor[part, low + LANE : high] = jnp.zeros((size, high - low - LANE), jnp.bfloat16)
    loads[2].wait()
    for i in range(blocks):
        part = pl.ds(i * size, size)
        mask = jnp.broadcast_to(link_mask[i : i + 1, :], (size, features)).astype(jnp.bfloat16)
        link[part, :] = link[part, :] * mask
    loads[1].wait()
    def big(b):
        return pl.ds(pl.multiple_of(b * batch, batch), batch)

    def first_terms(here):
        given_rows = given[here, :].astype(jnp.bfloat16)
        forward = jnp.concatenate(
            [dot_nt(given_rows[:, : n + tile], factor[n : n + tile, : n + tile]) for n in tiles], axis=1
        )
        red[here, :] = (forward * pivot_ref[...]).astype(jnp.bfloat16)
        forward = forward.astype(jnp.bfloat16)
        for q, span in enumerate(spans):
            up_out[q, here, :] = dot_nt(forward, link[span, :]).astype(jnp.bfloat16)

    head_rows = rows if rows < batch else 0

    def send_terms(p):
        for q in range(CHUNKS):
            send(p, q, True)

    @pl.when(bottom)
    def _():
        if head_rows:
            first_terms(pl.ds(0, head_rows))

    pl.semaphore_wait(barrier, greeted)

    @pl.when(top)
    def _():
        for load in above_loads:
            load.wait()

        @pl.when(has_left)
        def _():
            above_copy().start()

    @pl.when(bottom)
    def _():
        for p in range(head_rows // rows):
            send_terms(p)
        first_terms(pl.ds(head_rows, batch - head_rows))
        for p in range(head_rows // rows, batch // rows):
            send_terms(p)

        def first(b, carry):
            first_terms(big(b))
            for p in range(batch // rows):
                send_terms(b * (batch // rows) + p)
            return carry

        lax.fori_loop(1, total // batch, first, 0)

    for n in tiles:
        gain[:, n : n + tile] = dot_nn(link[:, n:], factor[n:, n : n + tile]).astype(jnp.bfloat16)

    @pl.when(middle)
    def _():
        for m in tiles:
            for n in tiles:
                gain_t[n : n + tile, m : m + tile] = gain[m : m + tile, n : n + tile].T

    @pl.when(has_down)
    def _():
        for m in tiles:
            for n in tiles:
                if m >= n:
                    turned = factor[m : m + tile, n : n + tile].T
                    scaled = turned.astype(jnp.float32) * pivot_ref[:, m : m + tile]
                    scaled_t[n : n + tile, m : m + tile] = scaled.astype(jnp.bfloat16)
        for m in tiles:
            for n in tiles:
                k = max(m, n)
                inner[m : m + tile, n : n + tile] = dot_nn(
                    scaled_t[m : m + tile, k:], factor[k:, n : n + tile]
                ).astype(jnp.bfloat16)

    @pl.when(bottom)
    def _():
        def own_part(b, carry):
            here = big(b)
            kept[here, :] = jnp.concatenate([dot_nn(red[here, n:], factor[n:, n : n + tile]) for n in tiles], axis=1)
            return carry

        lax.fori_loop(0, total // batch, own_part, 0)

    own_offset = offsets_ref[s, j]
    below = jnp.minimum(s + 1, levels - 1)
    from_own = (offsets_ref[below, j] == 0).astype(jnp.float32)
    from_side = (offsets_ref[below, jnp.maximum(j - 1, 0)] == 1).astype(jnp.float32)
    parent_own = (own_offset == 0).astype(jnp.float32)
    parent_side = (own_offset == 1).astype(jnp.float32)

    def parent_rows(q, here):
        return (
            dn_own[q, here, :].astype(jnp.float32) * parent_own
            + dn_side[q, here, :].astype(jnp.float32) * parent_side
        ).astype(jnp.bfloat16)

    def incoming_rows(q, here):
        return up_own[q, here, :].astype(jnp.float32) * from_own + up_side[q, here, :].astype(jnp.float32) * from_side

    @pl.when(top)
    def _():
        @pl.when(has_right)
        def _():
            above_copy().wait_recv()

        def own_part(b, carry):
            here = big(b)
            parents = jnp.concatenate([parent_rows(q, here) for q in range(CHUNKS)], axis=1)
            kept[here, :] = dot_nn(given[here, :].astype(jnp.bfloat16), inner[...]) - dot_nn(parents, gain[...])
            return carry

        lax.fori_loop(0, total // batch, own_part, 0)

    def product(chunk_of, matrix, use):
        begun = None
        for q, span in enumerate(spans):
            given_chunk = chunk_of(q)
            if q < CHUNKS - 1:
                partial = dot_nn(given_chunk, matrix[span, :])
                begun = partial if begun is None else begun + partial
            else:
                for n, columns in enumerate(spans):
                    result = dot_nn(given_chunk, matrix[span, columns])
                    use(n, columns, result if begun is None else begun[:, columns] + result)

    def wait_side(relay, exists, p, q):
        @pl.when(exists)
        def _():
            relay(p * CHUNKS + q).wait_recv()

    def forward_top(p):
        here = piece(p)

        def chunk_of(q):
            wait_side(up_relay, has_left, p, q)
            return incoming_rows(q, here).astype(jnp.bfloat16)

        def use(n, columns, value):
            result = kept[here, columns] - value
            dn_out[n, here, :] = result.astype(jnp.bfloat16)
            send(p, n, False)
            out_ref[here, columns] = result

        product(chunk_of, inner, use)

    def forward(p):
        here = piece(p)

        def chunk_of(q):
            wait_side(up_relay, has_left, p, q)
            reduced = (given[here, spans[q]] - incoming_rows(q, here)).astype(jnp.bfloat16)
            red[here, spans[q]] = reduced
            return reduced

        def use(n, columns, value):
            up_out[n, here, :] = value.astype(jnp.bfloat16)
            send(p, n, True)

        product(chunk_of, gain_t, use)

    def backward(p):
        here = piece(p)

        def chunk_of(q):
            wait_side(dn_relay, has_right, p, q)
            return parent_rows(q, here)

        def use(n, columns, value):
            result = kept[here, columns] - value

            @pl.when(has_down)
            def _():
                dn_out[n, here, :] = result.astype(jnp.bfloat16)
                send(p, n, False)

            out_ref[here, columns] = result

        product(chunk_of, gain, use)

    def relay_up(m):
        up_copy(m).wait_recv()

        @pl.when(has_right)
        def _():
            up_relay(m).start()

    def relay_down(m):
        dn_copy(m).wait_recv()

        @pl.when(has_left)
        def _():
            dn_relay(m).start()

    def forward_any(p):
        @pl.when(top)
        def _():
            forward_top(p)

        @pl.when(middle)
        def _():
            forward(p)

    def pass_up(n):
        m = routed_message(True, n)
        up_detour(m).wait_recv()
        up_on(m).start()

    def pass_down(n):
        m = routed_message(False, n)
        dn_detour(m).wait_recv()
        dn_on(m).start()

    def own_part_of(g):
        here = big(g)
        kept[here, :] = dot_nn(red[here, :], inner[...])

    acts = {RELAY_UP: relay_up, RELAY_DOWN: relay_down, FORWARD: forward_any, BACKWARD: backward}
    acts[OWN] = own_part_of
    if any(dst < src for src, dst, _, _ in ROUTES):
        acts[PASS_UP] = pass_up
    if any(dst > src for src, dst, _, _ in ROUTES):
        acts[PASS_DOWN] = pass_down

    def act_on(kinds, kind, counts):
        if len(kinds) == 1:
            acts[kinds[0]](counts[kinds[0]])
            return
        left, right = kinds[: len(kinds) // 2], kinds[len(kinds) // 2 :]

        @pl.when(kind < right[0])
        def _():
            act_on(left, kind, counts)

        @pl.when(kind >= right[0])
        def _():
            act_on(right, kind, counts)

    used = sorted(acts)

    def turn(i, carry):
        word, counts = carry
        kind = lax.rem(word, KINDS)
        act_on(used, kind, dict(zip(used, counts)))
        return lax.div(word, KINDS), tuple(jnp.where(kind == which, c + 1, c) for which, c in zip(used, counts))

    def block(w, counts):
        word = words[0]
        for i in range(1, len(words)):
            word = jnp.where(w == i, words[i], word)
        return lax.fori_loop(0, jnp.minimum(turns - w * DIGITS, DIGITS), turn, (word, counts))[1]

    lax.fori_loop(0, lax.div(turns + DIGITS - 1, DIGITS), block, tuple(jnp.int32(0) for _ in used))

    def finish(m, carry):
        @pl.when(has_up)
        def _():
            up_copy(m).wait_send()

            @pl.when(has_left)
            def _():
                dn_relay(m).wait_send()

        @pl.when(has_down)
        def _():
            dn_copy(m).wait_send()

            @pl.when(has_right)
            def _():
                up_relay(m).wait_send()

        if PASS_UP in acts:

            @pl.when(routed(origin, True, lax.div(m, CHUNKS)))
            def _():
                up_on(m).wait_send()

        if PASS_DOWN in acts:

            @pl.when(routed(origin, False, lax.div(m, CHUNKS)))
            def _():
                dn_on(m).wait_send()

        return carry

    lax.fori_loop(0, pieces * CHUNKS, finish, 0)

    @pl.when(top & has_left)
    def _():
        above_copy().wait_send()


def local(
    right_side,
    inverse_raw,
    inverse_pattern,
    coupling,
    coupling_pattern,
    pivots,
    offsets,
    above_solution,
):
    levels = lax.axis_size("section")
    nodes = lax.axis_size("scen")
    total, features = right_side.shape[2:]
    pieces = total // min(ROWS, total)
    vmem = pl.BlockSpec(memory_space=pltpu.VMEM)
    hbm = pl.BlockSpec(memory_space=pl.ANY)
    half = pltpu.VMEM((total, features), jnp.bfloat16)
    chunked = pltpu.VMEM((CHUNKS, total, features // CHUNKS), jnp.bfloat16)
    whole = pltpu.VMEM((total, features), jnp.float32)
    square = pltpu.VMEM((features, features), jnp.bfloat16)
    sems = pltpu.SemaphoreType.DMA((2, pieces * CHUNKS))
    solved = pl.pallas_call(
        functools.partial(kernel, levels, nodes),
        out_shape=pltpu.VMEM((total, features), jnp.float32),
        in_specs=[hbm] * 8,
        out_specs=vmem,
        scratch_shapes=[whole]
        + [square] * 6
        + [whole]
        + [half]
        + [chunked] * 8
        + [
            pltpu.VMEM(inverse_pattern.shape[2:], jnp.int32),
            pltpu.VMEM(coupling_pattern.shape[2:], jnp.int32),
            pltpu.VMEM((1, features), jnp.float32),
            pltpu.SMEM(offsets.shape, jnp.int32),
        ]
        + [pltpu.SemaphoreType.DMA((8,))]
        + [sems] * 6
        + [pltpu.SemaphoreType.DMA((2 + CHUNKS,))],
        compiler_params=pltpu.CompilerParams(
            collective_id=0, has_side_effects=True, vmem_limit_bytes=60 * 1024 * 1024
        ),
    )(
        right_side[0, 0],
        inverse_raw[0, 0],
        inverse_pattern[0, 0],
        coupling[0, 0],
        coupling_pattern[0, 0],
        pivots[0],
        offsets,
        above_solution[0],
    )
    return solved[None, None]


def solution(mesh):
    placed = (
        P("section", "scen", None, None),
        P("section", "scen", None, None),
        P("section", "scen", None, None),
        P("section", "scen", None, None),
        P("section", "scen", None, None),
        P("section", "scen", None),
        P(),
        P("scen", None, None),
    )
    return jax.shard_map(
        local,
        mesh=mesh,
        in_specs=placed,
        out_specs=P("section", "scen", None, None),
        check_vma=False,
    )
```
